32 devices in a mesh: row: 4 (over y, core), col: 4 (over z), dev: 2 (over x).
Axes of the slice: x: 2, y: 2, z: 4, core: 2. Of those that a mesh axis runs over, the one named last changes fastest.
Arguments:
- iterate: bfloat16 [64, 4, 4, 1024], P('dev', 'row', 'col'), may hold values from -6 to 6
- right_side: bfloat16 [64, 4, 4, 1024], P('dev', 'row', 'col'), may hold values from -6 to 6
- kernel: bfloat16 [2559], replicated, may hold values from -0.15625 to 0.15625
- inverse_rows: bfloat16 [4, 4, 1024, 1536], P('row', 'col'), may hold values from -0.1875 to 0.1875
- coarse_inverse: bfloat16 [512, 512], P('col', ('row', 'dev')), may hold values from -0.046875 to 0.046875
- aggregate: int32 [4, 4, 1024], P('row', 'col'), may hold values from 0 to 31
- send_index: int32 [4, 4, 4, 128], P('row', 'col'), may hold values from 0 to 1023
Outputs:
- correction: bfloat16 [64, 4, 4, 1024], P('dev', 'row', 'col')
The draws below stay inside these ranges and needn't reach their ends.
Inputs may be any that keep to these rules, and one draw needn't show every extreme that they name: `send_index`: repeats may occur within one list.
All inputs are finite; a program needn't handle non-finite values.
Results may differ from the reference program's by a relative error of at most 0.0057.
Values may be sent and summed in bfloat16 or wider, within the bound.
No kernel may reach another device: no remote copies, remote signals or barrier semaphores. Data moves between devices by JAX's collectives and lax.ppermute only.
A program may use at most 64 MiB of HBM per device.

```python
import jax
import jax.numpy as jnp
from jax import lax

PATCH = 1536
SHELL = 128
NK = 32
CORE = 1024
NBX = 4
NBY = 4
RHS = 64
COARSE = 512
N_DEV = 2


def set_ends(array, own_key, smallest, top_value):
    longest = array.shape.index(max(array.shape))
    spots = []
    for shift in (0, 1):
        where = [jax.random.randint(jax.random.fold_in(own_key, axis), (), 0, length) for axis, length in enumerate(array.shape)]
        where[longest] = (where[longest] + shift) % array.shape[longest]
        spots.append(tuple(where))
    return array.at[spots[0]].set(smallest).at[spots[1]].set(top_value)


def steps_of(rng, extent, split, smallest, largest):
    def one(axis_at, blocks):
        heights = jax.random.uniform(jax.random.fold_in(jax.random.fold_in(rng, 6), axis_at), (blocks,), jnp.float32, smallest / len(split), largest / len(split))
        return jnp.repeat(jnp.exp(heights), extent[axis_at] // blocks).reshape((-1,) + (1,) * (len(extent) - axis_at - 1))

    level = one(*split[0])
    for cut in split[1:]:
        level = level * one(*cut)
    return level


def centred(own_key, dims, spread, bound, cuts=(), dtype=jnp.bfloat16):
    entries = jax.random.normal(own_key, dims, jnp.float32) * spread
    if len(cuts) > 0:
        entries = steps_of(own_key, dims, cuts, -0.22, 0.18) * entries
    return jnp.clip(entries, min=-bound, max=bound).astype(dtype)


def setup_inputs(seed: int = 0) -> dict:
    key_list = jax.random.split(jax.random.key(seed), 8)
    return {
        "iterate": centred(key_list[0], (RHS, NBX, NBY, CORE), 1.0, 6.0, ((0, 2), (1, 4), (2, 4))),
        "right_side": centred(key_list[1], (RHS, NBX, NBY, CORE), 1.0, 6.0, ((0, 2), (1, 4), (2, 4))),
        "kernel": centred(key_list[2], (CORE + PATCH - 1,), PATCH ** -0.5, 0.15625),
        "inverse_rows": centred(key_list[3], (NBX, NBY, CORE, PATCH), CORE ** -0.5, 0.1875, ((0, 4), (1, 4))),
        "coarse_inverse": centred(key_list[4], (COARSE, COARSE), (COARSE * CORE // NK) ** -0.5, 0.046875, ((0, 4), (1, 8))),
        "aggregate": set_ends(jax.random.randint(key_list[5], (NBX, NBY, CORE), 0, NK), jax.random.fold_in(key_list[5], 1), 0, NK - 1).astype(jnp.int32),
        "send_index": set_ends(jax.random.randint(key_list[6], (NBX, NBY, 4, SHELL), 0, CORE), jax.random.fold_in(key_list[6], 1), 0, CORE - 1).astype(jnp.int32),
    }


def reference(iterate, right_side, kernel, inverse_rows, coarse_inverse, aggregate, send_index):
    n_rhs, n_bx, n_by, n_core = iterate.shape
    n_shell = send_index.shape[3]
    n_patch = inverse_rows.shape[3]
    sent = []
    for direction in range(4):
        positions = jnp.broadcast_to(send_index[None, :, :, direction, :], (n_rhs, n_bx, n_by, n_shell))
        sent.append(jnp.take_along_axis(iterate, positions, axis=3))
    shells = [jnp.roll(sent[0], 1, axis=1), jnp.roll(sent[1], -1, axis=1),
              jnp.roll(sent[2], 1, axis=2), jnp.roll(sent[3], -1, axis=2)]
    patch = jnp.concatenate([iterate] + shells, axis=3)
    offsets = (jnp.arange(n_patch).astype(jnp.int32)[:, None] - jnp.arange(n_core).astype(jnp.int32)[None, :] + (n_core - 1)).astype(jnp.int32)
    toeplitz = kernel[offsets]
    field = jnp.dot(patch.reshape(-1, n_patch), toeplitz, preferred_element_type=jnp.float32)
    field = field.reshape(n_rhs, n_bx, n_by, n_core)
    residual = (right_side.astype(jnp.float32) - iterate.astype(jnp.float32) - field).astype(jnp.bfloat16)

    def local_solve(pair):
        rows_here, inverse_here = pair
        return jnp.einsum("ryi,yip->ryp", rows_here.astype(jnp.float32), inverse_here.astype(jnp.float32)).astype(jnp.bfloat16)

    local = jnp.moveaxis(lax.map(local_solve, (jnp.moveaxis(residual, 1, 0), inverse_rows)), 0, 1)
    grid_x = jnp.broadcast_to(jnp.arange(n_bx).astype(jnp.int32)[:, None, None], (n_bx, n_by, n_core))
    grid_y = jnp.broadcast_to(jnp.arange(n_by).astype(jnp.int32)[None, :, None], (n_bx, n_by, n_core))
    coarse = jnp.zeros((n_rhs, n_bx, n_by, NK), jnp.float32)
    coarse = coarse.at[:, grid_x, grid_y, aggregate].add(residual.astype(jnp.float32)).astype(jnp.bfloat16)
    coarse_flat = jnp.transpose(coarse, (0, 2, 1, 3)).reshape(n_rhs, -1)
    solved = jnp.dot(coarse_flat, coarse_inverse, preferred_element_type=jnp.float32)
    solved = solved.reshape(n_rhs, n_bx, N_DEV, n_by, NK // N_DEV)
    solved = jnp.transpose(solved, (0, 1, 3, 2, 4)).reshape(n_rhs, n_bx, n_by, NK)
    lookup = jnp.broadcast_to(aggregate[None], (n_rhs, n_bx, n_by, n_core))
    coarse_part = jnp.take_along_axis(solved, lookup, axis=3)
    returned = local[..., n_core:].astype(jnp.float32).reshape(n_rhs, n_bx, n_by, 4, n_shell)
    arrivals = [jnp.roll(returned[:, :, :, 0], -1, axis=1), jnp.roll(returned[:, :, :, 1], 1, axis=1),
                jnp.roll(returned[:, :, :, 2], -1, axis=2), jnp.roll(returned[:, :, :, 3], 1, axis=2)]
    total = local[..., :n_core].astype(jnp.float32) + coarse_part
    shell_x = jnp.broadcast_to(jnp.arange(n_bx).astype(jnp.int32)[:, None, None], (n_bx, n_by, n_shell))
    shell_y = jnp.broadcast_to(jnp.arange(n_by).astype(jnp.int32)[None, :, None], (n_bx, n_by, n_shell))
    for direction in range(4):
        total = total.at[:, shell_x, shell_y, send_index[:, :, direction, :]].add(arrivals[direction])
    return total.astype(jnp.bfloat16)
```

```python
import functools

import jax
import jax.numpy as jnp
from jax import lax
from jax.experimental import pallas as pl
from jax.experimental.pallas import tpu as pltpu
from jax.sharding import PartitionSpec as P

LANES = 128
BLOCK = 256
VMEM = pl.BlockSpec(memory_space=pltpu.VMEM)
HBM = pl.BlockSpec(memory_space=pltpu.HBM)
F32 = jnp.float32
BF16 = jnp.bfloat16


def mm(left, right):
    return jnp.dot(left, right, preferred_element_type=F32)


def mm_nt(left, right):
    return lax.dot_general(left, right, (((1,), (1,)), ((), ())), preferred_element_type=F32)


def one_hot(labels, rows):
    shape = (rows, labels.shape[1])
    hit = lax.broadcasted_iota(jnp.int32, shape, 0) == jnp.broadcast_to(labels, shape)
    return jnp.where(hit, 1.0, 0.0).astype(BF16)


def place(axis):
    index = lax.axis_index(axis)
    return index, lax.rem(index, 2), lax.axis_size(axis)


def partners(axis):
    index, odd, count = place(axis)
    outer = lax.rem(index + jnp.where(odd == 1, 1, count - 1), count)
    inner = index + jnp.where(odd == 1, -1, 1)
    return [index, outer, inner] + [lax.rem(index + o, count) for o in range(2, count - 1)]


def outer_pairs(count):
    return [(i, (i + 1) % count if i % 2 else (i - 1) % count) for i in range(count)]


def inner_pairs(count):
    return [(i, i ^ 1) for i in range(count)]


def shifted(count, step):
    return [(i, (i + step) % count) for i in range(count)]


def gather_kernel(own_hbm, send_hbm, right_hbm, labels_hbm, columns_hbm, co, ro, ci, ri, spots_ref, own_ref, right_ref, labels_ref, columns_ref, send_ref, sems):
    pairs = (
        (send_hbm, send_ref),
        (own_hbm, own_ref),
        (right_hbm, right_ref),
        (labels_hbm, labels_ref),
        (columns_hbm, columns_ref),
    )
    copies = [pltpu.make_async_copy(a, b, sems.at[i]) for i, (a, b) in enumerate(pairs)]
    for copy in copies:
        copy.start()
    copies[0].wait()
    n_core = own_ref.shape[1]
    shell = send_ref.shape[1]
    hots = []
    for slot, (axis, base, inner) in enumerate((("row", 0, 0), ("row", 0, 1), ("col", 2, 0), ("col", 2, 1))):
        odd = place(axis)[1]
        direction = base + jnp.where(odd == 1, inner, 1 - inner)
        hot = one_hot(send_ref[pl.ds(direction, 1), :], n_core)
        spots_ref[:, slot * shell : (slot + 1) * shell] = hot
        hots.append(hot)
    copies[1].wait()
    own = own_ref[...]
    for slot, out in ((2, co), (0, ro), (3, ci), (1, ri)):
        out[...] = mm(own, spots_ref[:, slot * shell : (slot + 1) * shell]).astype(BF16)
    for copy in copies[2:]:
        copy.wait()


def strip_kernel(kernel_ref, own_ref, right_ref, inv_hbm, strip_ref, base_ref, inv_ref, sem):
    copy = pltpu.make_async_copy(inv_hbm, inv_ref, sem)
    copy.start()
    width = kernel_ref.shape[1]
    n_core = own_ref.shape[1]
    rows = 16
    row = jnp.broadcast_to(kernel_ref[...], (rows, width))
    first = pltpu.roll(row, 0, 1, stride=1, stride_axis=0)
    for g in range(BLOCK // rows):
        part = first if g == 0 else pltpu.roll(first, g * rows, 1)
        strip_ref[g * rows : (g + 1) * rows, :] = part[:, BLOCK:].astype(BF16)
    own = own_ref[...]
    for b in range(n_core // BLOCK):
        start = n_core - BLOCK - BLOCK * b
        here = slice(b * BLOCK, (b + 1) * BLOCK)
        field = mm_nt(own, strip_ref[:, start : start + n_core])
        base_ref[:, here] = right_ref[:, here].astype(F32) - own[:, here].astype(F32) - field
    copy.wait()


def columns_kernel(labels_ref, *refs):
    n_dev = len(refs) - 2
    parts, columns_ref, member_ref = refs[:n_dev], refs[n_dev], refs[n_dev + 1]
    targets = partners("col")
    half = parts[0].shape[0] // len(targets)
    dev = lax.axis_index("dev")
    columns_ref[...] = jnp.zeros_like(columns_ref)
    for d, by in enumerate(targets):
        source = pl.multiple_of(by * half, half)
        for e in range(n_dev):
            target = pl.multiple_of(lax.rem(dev + e, n_dev) * half, half)
            columns_ref[d, pl.ds(target, half), :] = parts[e][pl.ds(source, half), :]
    member_ref[...] = one_hot(labels_ref[...], member_ref.shape[0])


def residual_kernel(base_ref, to, ti, uo, ui, strip_ref, inv_ref, member_ref, ro, rx, ri, co, ci, res_ref):
    n_core = base_ref.shape[1]
    rows, shell = to.shape
    odd_row, odd_col = place("row")[1] == 1, place("col")[1] == 1
    low = [jnp.where(odd_row, ti[...], to[...]), jnp.where(odd_row, to[...], ti[...])]
    high = [jnp.where(odd_col, ui[...], uo[...]), jnp.where(odd_col, uo[...], ui[...])]
    shells = jnp.concatenate(low + high, axis=1)
    width = shells.shape[1]
    for b in range(n_core // BLOCK):
        start = 2 * n_core - BLOCK - BLOCK * b
        here = slice(b * BLOCK, (b + 1) * BLOCK)
        field = mm_nt(shells, strip_ref[:, start : start + width])
        res_ref[:, here] = (base_ref[:, here] - field).astype(BF16)
    res = res_ref[...]
    coarse = mm_nt(res, member_ref[...]).astype(BF16)
    rx[...] = coarse
    local = mm(res, inv_ref[:, n_core:]).astype(BF16)
    back = [local[:, j * shell : (j + 1) * shell] for j in range(4)]
    ro[:rows, :] = jnp.where(odd_row, back[1], back[0])
    ro[rows:, :] = coarse
    ri[:rows, :] = jnp.where(odd_row, back[0], back[1])
    ri[rows:, :] = coarse
    co[...] = jnp.where(odd_col, back[3], back[2])
    ci[...] = jnp.where(odd_col, back[2], back[3])


def partial_kernel(columns_ref, co, ci, *refs):
    sources = partners("row")
    n_bx = len(sources)
    gathered, outs = refs[:n_bx], refs[n_bx:]
    width = columns_ref.shape[2]
    rows = co.shape[0]
    total = jnp.zeros((rows, width), F32)
    for bx, ref in zip(sources, gathered):
        piece = ref[-rows:, :].astype(F32)
        if width > LANES:
            piece = jnp.concatenate([piece, jnp.zeros((rows, width - LANES), F32)], axis=1)
        total = total + pltpu.roll(piece, bx * (width // n_bx), 1)
    total = total.astype(BF16)
    outs[1][:rows, :] = co[...].astype(F32)
    outs[2][:rows, :] = ci[...].astype(F32)
    for d, out in enumerate(outs):
        out[-rows:, :] = mm_nt(total, columns_ref[d])


def local_kernel(res_ref, inv_ref, spots_ref, ro, ri, acc_ref):
    rows, n_core = res_ref.shape
    arrived = jnp.concatenate([ro[:rows, :], ri[:rows, :]], axis=1)
    added = mm_nt(arrived, spots_ref[:, : arrived.shape[1]])
    acc_ref[...] = mm(res_ref[...], inv_ref[:, :n_core]).astype(BF16).astype(F32) + added


def final_kernel(acc_ref, member_ref, spots_ref, *refs):
    parts, out_ref = refs[:-1], refs[-1]
    rows = acc_ref.shape[0]
    solved = parts[0][...]
    for part in parts[1:]:
        solved = solved + part[-rows:, :]
    high = solved.astype(BF16)
    low = (solved - high.astype(F32)).astype(BF16)
    both = mm(jnp.concatenate([high, low], axis=0), member_ref[...])
    arrived = jnp.concatenate([parts[1][:rows, :], parts[2][:rows, :]], axis=1).astype(BF16)
    added = mm_nt(arrived, spots_ref[:, arrived.shape[1] :])
    out_ref[...] = (acc_ref[...] + added + both[:rows] + both[rows:]).astype(BF16)


def call(body, name, shapes, *args, hbm=(), scratch=(), limit=16, flops=10**6):
    out_shape = [jax.ShapeDtypeStruct(s, t) for s, t in shapes]
    size = sum(a.size * a.dtype.itemsize for a in args)
    return pl.pallas_call(
        body,
        out_shape=out_shape,
        in_specs=[HBM if i in hbm else VMEM for i in range(len(args))],
        out_specs=[VMEM] * len(out_shape),
        scratch_shapes=scratch,
        name=name,
        compiler_params=pltpu.CompilerParams(vmem_limit_bytes=limit << 20),
        cost_estimate=pl.CostEstimate(flops=flops, bytes_accessed=size, transcendentals=0),
    )(*args)


def per_device(iterate, right_side, kernel, inverse_rows, coarse_inverse, aggregate, send_index):
    own = iterate[:, 0, 0, :]
    right = right_side[:, 0, 0, :]
    inverse = inverse_rows[0, 0]
    labels = aggregate[0]
    send = send_index[0, 0]
    mine = coarse_inverse.T
    rows, n_core = own.shape
    n_shell = send.shape[1]
    n_patch = inverse.shape[1]
    n_bx, n_by, n_dev = (lax.axis_size(a) for a in ("row", "col", "dev"))
    coarse_rows = coarse_inverse.shape[0]
    shell = ((rows, n_shell), BF16)
    double = ((2 * rows, LANES), BF16)

    same = [(a.shape, a.dtype) for a in (own, right, labels, mine)]
    co, ro, ci, ri, spots, own, right, labels, mine = call(
        gather_kernel,
        "gather",
        [shell] * 4 + [((n_core, 4 * n_shell), BF16)] + same,
        own,
        send,
        right,
        labels,
        mine,
        hbm=range(5),
        scratch=[pltpu.VMEM(send.shape, send.dtype), pltpu.SemaphoreType.DMA((5,))],
    )
    uo = lax.ppermute(co, "col", outer_pairs(n_by))
    to = lax.ppermute(ro, "row", outer_pairs(n_bx))
    ui = lax.ppermute(ci, "col", inner_pairs(n_by))
    ti = lax.ppermute(ri, "row", inner_pairs(n_bx))
    halves = [mine] + [lax.ppermute(mine, "dev", shifted(n_dev, -e)) for e in range(1, n_dev)]

    width = n_core + n_patch
    padded = jnp.pad(kernel.astype(F32), (1, width - kernel.shape[0] - 1))[None, :]
    strip, base, inverse = call(
        strip_kernel,
        "strip",
        [((BLOCK, width - BLOCK), BF16), ((rows, n_core), F32), (inverse.shape, BF16)],
        padded,
        own,
        right,
        inverse,
        hbm=(3,),
        scratch=[pltpu.SemaphoreType.DMA],
    )
    columns, member = call(
        columns_kernel,
        "columns",
        [((n_by, LANES, coarse_rows), BF16), ((LANES, n_core), BF16)],
        labels,
        *halves,
    )
    ro, rx, ri, co, ci, res = call(
        residual_kernel,
        "residual",
        [double, shell, double, shell, shell, ((rows, n_core), BF16)],
        base,
        to,
        ti,
        uo,
        ui,
        strip,
        inverse,
        member,
    )
    ao = lax.ppermute(ro, "row", outer_pairs(n_bx))
    rest = [lax.ppermute(rx, "row", shifted(n_bx, -o)) for o in range(2, n_bx - 1)]
    ai = lax.ppermute(ri, "row", inner_pairs(n_bx))
    single, wide = ((rows, LANES), F32), ((2 * rows, LANES), F32)
    partials = call(
        partial_kernel,
        "partial",
        [single, wide, wide] + [single] * (n_by - 3),
        columns,
        co,
        ci,
        rx,
        ao,
        ai,
        *rest,
    )
    so = lax.ppermute(partials[1], "col", outer_pairs(n_by))
    others = [lax.ppermute(partials[d + 1], "col", shifted(n_by, d)) for d in range(2, n_by - 1)]
    si = lax.ppermute(partials[2], "col", inner_pairs(n_by))
    (acc,) = call(local_kernel, "local", [((rows, n_core), F32)], res, inverse, spots, ao, ai)
    (out,) = call(final_kernel, "final", [((rows, n_core), BF16)], acc, member, spots, partials[0], so, si, *others)
    return out[:, None, None, :]


def solution(mesh):
    in_specs = (
        P("dev", "row", "col", None),
        P("dev", "row", "col", None),
        P(),
        P("row", "col", None, None),
        P("col", ("row", "dev")),
        P("row", "col", None),
        P("row", "col", None, None),
    )
    out_specs = P("dev", "row", "col", None)
    return jax.shard_map(
        per_device, mesh=mesh, in_specs=in_specs, out_specs=out_specs, check_vma=False
    )
```

```python
import functools

import jax
import jax.numpy as jnp
from jax import lax
from jax.experimental import pallas as pl
from jax.experimental.pallas import tpu as pltpu
from jax.sharding import PartitionSpec as P


LANES = 128
BLOCK = 256
VMEM = pl.BlockSpec(memory_space=pltpu.VMEM)
HBM = pl.BlockSpec(memory_space=pltpu.HBM)
F32 = jnp.float32
BF16 = jnp.bfloat16


def mm(left, right):
    return jnp.dot(left, right, preferred_element_type=F32)


def mm_nt(left, right):
    return lax.dot_general(left, right, (((1,), (1,)), ((), ())), preferred_element_type=F32)


def one_hot(labels, rows):
    shape = (rows, labels.shape[1])
    hit = lax.broadcasted_iota(jnp.int32, shape, 0) == jnp.broadcast_to(labels, shape)
    return jnp.where(hit, 1.0, 0.0).astype(BF16)


def place(axis):
    index = lax.axis_index(axis)
    return index, lax.rem(index, 2), lax.axis_size(axis)


def partners(axis):
    index, odd, count = place(axis)
    outer = lax.rem(index + jnp.where(odd == 1, 1, count - 1), count)
    inner = index + jnp.where(odd == 1, -1, 1)
    return [index, outer, inner] + [lax.rem(index + o, count) for o in range(2, count - 1)]


def outer_pairs(count):
    return [(i, (i + 1) % count if i % 2 else (i - 1) % count) for i in range(count)]


def inner_pairs(count):
    return [(i, i ^ 1) for i in range(count)]


def shifted(count, step):
    return [(i, (i + step) % count) for i in range(count)]


def gather_kernel(send_hbm, own_hbm, *refs):
    rest = (len(refs) - 8) // 2
    more_hbm, (co, ro, ci, ri, spots_ref, own_ref) = refs[:rest], refs[rest : rest + 6]
    more, (send_ref, sems) = refs[rest + 6 : -2], refs[-2:]
    pairs = zip((send_hbm, own_hbm, *more_hbm), (send_ref, own_ref, *more))
    copies = [pltpu.make_async_copy(a, b, sems.at[i]) for i, (a, b) in enumerate(pairs)]
    for copy in copies:
        copy.start()
    copies[0].wait()
    n_core = own_ref.shape[1]
    shell = send_ref.shape[1]
    hots = []
    for slot, (axis, base, inner) in enumerate((("row", 0, 0), ("row", 0, 1), ("col", 2, 0), ("col", 2, 1))):
        odd = place(axis)[1]
        direction = base + jnp.where(odd == 1, inner, 1 - inner)
        hot = one_hot(send_ref[pl.ds(direction, 1), :], n_core)
        spots_ref[:, slot * shell : (slot + 1) * shell] = hot
        hots.append(hot)
    copies[1].wait()
    own = own_ref[...]
    for slot, out in ((2, co), (0, ro), (3, ci), (1, ri)):
        out[...] = mm(own, spots_ref[:, slot * shell : (slot + 1) * shell]).astype(BF16)
    for copy in copies[2:]:
        copy.wait()


def strip_kernel(kernel_ref, own_ref, right_ref, labels_ref, strip_ref, base_ref, member_ref):
    n_core = own_ref.shape[1]
    width = kernel_ref.shape[1]
    rows = 16
    row = jnp.broadcast_to(kernel_ref[...], (rows, width))
    first = pltpu.roll(row, 0, 1, stride=1, stride_axis=0)
    for g in range(BLOCK // rows):
        part = first if g == 0 else pltpu.roll(first, g * rows, 1)
        strip_ref[g * rows : (g + 1) * rows, :] = part[:, BLOCK:].astype(BF16)
    own = own_ref[...]
    for b in range(n_core // BLOCK):
        start = n_core - BLOCK - BLOCK * b
        here = slice(b * BLOCK, (b + 1) * BLOCK)
        field = mm_nt(own, strip_ref[:, start : start + n_core])
        base_ref[:, here] = right_ref[:, here].astype(F32) - own[:, here].astype(F32) - field
    member_ref[...] = one_hot(labels_ref[...], member_ref.shape[0])


def columns_kernel(*refs):
    parts, columns_ref = refs[:-1], refs[-1]
    n_dev = len(parts)
    targets = partners("col")
    half = parts[0].shape[0] // len(targets)
    dev = lax.axis_index("dev")
    columns_ref[...] = jnp.zeros_like(columns_ref)
    for d, by in enumerate(targets):
        source = pl.multiple_of(by * half, half)
        for e in range(n_dev):
            target = pl.multiple_of(lax.rem(dev + e, n_dev) * half, half)
            columns_ref[d, pl.ds(target, half), :] = parts[e][pl.ds(source, half), :]


def residual_kernel(unknowns, base_ref, to, ti, uo, ui, strip_ref, inv_ref, member_ref, ro, rx, ri, co, ci, res_ref):
    n_core = base_ref.shape[1]
    rows, shell = to.shape
    odd_row, odd_col = place("row")[1] == 1, place("col")[1] == 1
    low = [jnp.where(odd_row, ti[...], to[...]), jnp.where(odd_row, to[...], ti[...])]
    high = [jnp.where(odd_col, ui[...], uo[...]), jnp.where(odd_col, uo[...], ui[...])]
    shells = jnp.concatenate(low + high, axis=1)
    width = shells.shape[1]
    for b in range(n_core // BLOCK):
        start = 2 * n_core - BLOCK - BLOCK * b
        here = slice(b * BLOCK, (b + 1) * BLOCK)
        field = mm_nt(shells, strip_ref[:, start : start + width])
        res_ref[:, here] = (base_ref[:, here] - field).astype(BF16)
    res = res_ref[...]
    coarse = pack(mm_nt(res, member_ref[...]), unknowns).astype(BF16)
    rx[...] = coarse
    local = mm(res, inv_ref[:, n_core:]).astype(BF16)
    back = [local[:, j * shell : (j + 1) * shell] for j in range(4)]
    ro[:rows, :] = jnp.where(odd_row, back[1], back[0])
    ro[rows:, :] = coarse
    ri[:rows, :] = jnp.where(odd_row, back[0], back[1])
    ri[rows:, :] = coarse
    co[...] = jnp.where(odd_col, back[3], back[2])
    ci[...] = jnp.where(odd_col, back[2], back[3])


def partial_kernel(unknowns, columns_ref, co, ci, *refs):
    sources = partners("row")
    n_bx = len(sources)
    gathered, outs = refs[:n_bx], refs[n_bx:]
    width = columns_ref.shape[2]
    rows = co.shape[0]
    height = gathered[0].shape[0]
    total = jnp.zeros((rows, width), F32)
    for bx, ref in zip(sources, gathered):
        piece = unpack(ref[-height:, :].astype(F32), unknowns)
        if width > LANES:
            piece = jnp.concatenate([piece, jnp.zeros((rows, width - LANES), F32)], axis=1)
        total = total + pltpu.roll(piece, bx * unknowns, 1)
    total = total.astype(BF16)
    outs[1][:rows, :] = co[...]
    outs[2][:rows, :] = ci[...]
    for d, out in enumerate(outs):
        part = pack(mm_nt(total, columns_ref[d]), unknowns)
        if d == 0:
            out[...] = part
        else:
            high = part.astype(BF16)
            out[-2 * height : -height, :] = high
            out[-height:, :] = (part - high.astype(F32)).astype(BF16)


def local_kernel(res_ref, inv_ref, spots_ref, ro, ri, acc_ref):
    rows, n_core = res_ref.shape
    arrived = jnp.concatenate([ro[:rows, :], ri[:rows, :]], axis=1)
    added = mm_nt(arrived, spots_ref[:, : arrived.shape[1]])
    acc_ref[...] = mm(res_ref[...], inv_ref[:, :n_core]).astype(BF16).astype(F32) + added


def final_kernel(unknowns, acc_ref, member_ref, spots_ref, *refs):
    parts, out_ref = refs[:-1], refs[-1]
    rows = acc_ref.shape[0]
    height = parts[0].shape[0]
    solved = parts[0][...]
    for part in parts[1:]:
        solved = solved + part[-2 * height : -height, :].astype(F32) + part[-height:, :].astype(F32)
    solved = unpack(solved, unknowns)
    high = solved.astype(BF16)
    low = (solved - high.astype(F32)).astype(BF16)
    both = mm(jnp.concatenate([high, low], axis=0), member_ref[...])
    arrived = jnp.concatenate([parts[1][:rows, :], parts[2][:rows, :]], axis=1)
    added = mm_nt(arrived, spots_ref[:, arrived.shape[1] :])
    out_ref[...] = (acc_ref[...] + added + both[:rows] + both[rows:]).astype(BF16)


def pack(value, unknowns):
    groups = LANES // unknowns
    height = value.shape[0] // groups
    parts = [pltpu.roll(value[q * height : (q + 1) * height, :], q * unknowns, 1) for q in range(1, groups)]
    return sum(parts, value[:height, :])


def unpack(packed, unknowns):
    keep = lax.broadcasted_iota(jnp.int32, packed.shape, 1) < unknowns
    parts = [packed] + [pltpu.roll(packed, LANES - q * unknowns, 1) for q in range(1, LANES // unknowns)]
    return jnp.concatenate([jnp.where(keep, part, 0.0) for part in parts], axis=0)


def call(body, shapes, *args, hbm=(), scratch=(), limit=16, flops=10**6):
    out_shape = [jax.ShapeDtypeStruct(s, t) for s, t in shapes]
    args = [pltpu.with_memory_space_constraint(a, pltpu.HBM) if i in hbm else a for i, a in enumerate(args)]
    size = sum(a.size * a.dtype.itemsize for a in args)
    return pl.pallas_call(
        body,
        out_shape=out_shape,
        in_specs=[HBM if i in hbm else VMEM for i in range(len(args))],
        out_specs=[VMEM] * len(out_shape),
        scratch_shapes=scratch,
        compiler_params=pltpu.CompilerParams(vmem_limit_bytes=limit << 20),
        cost_estimate=pl.CostEstimate(flops=flops, bytes_accessed=size, transcendentals=0),
    )(*args)


def per_device(iterate, right_side, kernel, inverse_rows, coarse_inverse, aggregate, send_index):
    own = iterate[:, 0, 0, :]
    right = right_side[:, 0, 0, :]
    inverse = inverse_rows[0, 0]
    labels = aggregate[0]
    send = send_index[0, 0]
    mine = coarse_inverse.T
    rows, n_core = own.shape
    n_shell = send.shape[1]
    n_patch = inverse.shape[1]
    n_bx, n_by, n_dev = (lax.axis_size(a) for a in ("row", "col", "dev"))
    coarse_rows = coarse_inverse.shape[0]
    shell = ((rows, n_shell), BF16)
    unknowns = coarse_rows // n_bx
    height = rows * unknowns // LANES
    double = ((rows + height, LANES), BF16)

    held = (own, right, labels, mine, kernel)
    co, ro, ci, ri, spots, own, right, labels, mine, kernel = call(
        gather_kernel,
        [shell] * 4 + [((n_core, 4 * n_shell), BF16)] + [(a.shape, a.dtype) for a in held],
        send,
        *held,
        hbm=range(6),
        flops=4 * 10**9,
        scratch=[pltpu.VMEM(send.shape, send.dtype), pltpu.SemaphoreType.DMA((6,))],
    )
    uo = lax.ppermute(co, "col", outer_pairs(n_by))
    to = lax.ppermute(ro, "row", outer_pairs(n_bx))
    ui = lax.ppermute(ci, "col", inner_pairs(n_by))
    ti = lax.ppermute(ri, "row", inner_pairs(n_bx))
    halves = [mine] + [lax.ppermute(mine, "dev", shifted(n_dev, -e)) for e in range(1, n_dev)]

    width = n_core + n_patch
    padded = jnp.pad(kernel.astype(F32), (1, width - kernel.shape[0] - 1))[None, :]
    strip, base, member = call(
        strip_kernel,
        [((BLOCK, width - BLOCK), BF16), ((rows, n_core), F32), ((LANES, n_core), BF16)],
        padded,
        own,
        right,
        labels,
    )
    ro, rx, ri, co, ci, res = call(
        functools.partial(residual_kernel, unknowns),
        [double, ((height, LANES), BF16), double, shell, shell, ((rows, n_core), BF16)],
        base,
        to,
        ti,
        uo,
        ui,
        strip,
        inverse,
        member,
    )
    ao = lax.ppermute(ro, "row", outer_pairs(n_bx))
    rest = [lax.ppermute(rx, "row", shifted(n_bx, -o)) for o in range(2, n_bx - 1)]
    ai = lax.ppermute(ri, "row", inner_pairs(n_bx))
    (columns,) = call(columns_kernel, [((n_by, LANES, coarse_rows), BF16)], *halves)
    single, wide = ((2 * height, LANES), BF16), ((rows + 2 * height, LANES), BF16)
    partials = call(
        functools.partial(partial_kernel, unknowns),
        [((height, LANES), F32), wide, wide] + [single] * (n_by - 3),
        columns,
        co,
        ci,
        rx,
        ao,
        ai,
        *rest,
    )
    so = lax.ppermute(partials[1], "col", outer_pairs(n_by))
    others = [lax.ppermute(partials[d + 1], "col", shifted(n_by, d)) for d in range(2, n_by - 1)]
    si = lax.ppermute(partials[2], "col", inner_pairs(n_by))
    (acc,) = call(local_kernel, [((rows, n_core), F32)], res, inverse, spots, ao, ai)
    (out,) = call(functools.partial(final_kernel, unknowns), [((rows, n_core), BF16)], acc, member, spots, partials[0], so, si, *others)
    return out[:, None, None, :]


def solution(mesh):
    in_specs = (
        P("dev", "row", "col", None),
        P("dev", "row", "col", None),
        P(),
        P("row", "col", None, None),
        P("col", ("row", "dev")),
        P("row", "col", None),
        P("row", "col", None, None),
    )
    out_specs = P("dev", "row", "col", None)

    return jax.shard_map(per_device, mesh=mesh, in_specs=in_specs, out_specs=out_specs, check_vma=False)
```

```python
import functools

import jax
import jax.numpy as jnp
from jax import lax
from jax.experimental import pallas as pl
from jax.experimental.pallas import tpu as pltpu
from jax.sharding import PartitionSpec as P


LANES = 128
BLOCK = 256
VMEM = pl.BlockSpec(memory_space=pltpu.VMEM)
HBM = pl.BlockSpec(memory_space=pltpu.HBM)
F32 = jnp.float32
BF16 = jnp.bfloat16


def mm(left, right):
    return jnp.dot(left, right, preferred_element_type=F32)


def mm_nt(left, right):
    return lax.dot_general(left, right, (((1,), (1,)), ((), ())), preferred_element_type=F32)


def one_hot(labels, rows):
    shape = (rows, labels.shape[1])
    hit = lax.broadcasted_iota(jnp.int16, shape, 0) == jnp.broadcast_to(labels.astype(jnp.int16), shape)
    return jnp.where(hit, jnp.ones(shape, BF16), jnp.zeros(shape, BF16))


def toeplitz(values, strip_ref, offset, blocks):
    rows, parts = values.shape[0], values.shape[1] // BLOCK
    stacked = jnp.concatenate([values[:, u * BLOCK : (u + 1) * BLOCK] for u in range(parts)], axis=0)
    starts = [offset + BLOCK * t for t in range(blocks - 1 + parts)]
    tiles = [mm_nt(stacked, strip_ref[:, start : start + BLOCK]) for start in starts]
    return [
        sum(tiles[blocks - 1 - b + u][u * rows : (u + 1) * rows] for u in range(parts)) for b in range(blocks)
    ]


def place(axis):
    index = lax.axis_index(axis)
    return index, lax.rem(index, 2), lax.axis_size(axis)


def partners(axis):
    index, odd, count = place(axis)
    outer = lax.rem(index + jnp.where(odd == 1, 1, count - 1), count)
    inner = index + jnp.where(odd == 1, -1, 1)
    return [index, outer, inner] + [lax.rem(index + o, count) for o in range(2, count - 1)]


def outer_pairs(count):
    return [(i, (i + 1) % count if i % 2 else (i - 1) % count) for i in range(count)]


def inner_pairs(count):
    return [(i, i ^ 1) for i in range(count)]


def shifted(count, step):
    return [(i, (i + step) % count) for i in range(count)]


def gather_kernel(send_hbm, own_hbm, *refs):
    rest = (len(refs) - 8) // 2
    more_hbm, (co, ro, ci, ri, spots_ref, own_ref) = refs[:rest], refs[rest : rest + 6]
    more, (send_ref, sems) = refs[rest + 6 : -2], refs[-2:]
    pairs = zip((send_hbm, own_hbm, *more_hbm), (send_ref, own_ref, *more))
    copies = [pltpu.make_async_copy(a, b, sems.at[i]) for i, (a, b) in enumerate(pairs)]
    for copy in copies:
        copy.start()
    copies[0].wait()
    n_core = own_ref.shape[1]
    shell = send_ref.shape[1]
    hots = []
    for slot, (axis, base, inner) in enumerate((("row", 0, 0), ("row", 0, 1), ("col", 2, 0), ("col", 2, 1))):
        odd = place(axis)[1]
        direction = base + jnp.where(odd == 1, inner, 1 - inner)
        hot = one_hot(send_ref[pl.ds(direction, 1), :], n_core)
        spots_ref[:, slot * shell : (slot + 1) * shell] = hot
        hots.append(hot)
    copies[1].wait()
    own = own_ref[...]
    for slot, out in ((2, co), (0, ro), (3, ci), (1, ri)):
        out[...] = mm(own, spots_ref[:, slot * shell : (slot + 1) * shell]).astype(BF16)
    for copy in copies[2:]:
        copy.wait()


def strip_kernel(kernel_ref, own_ref, right_ref, labels_ref, strip_ref, base_ref, member_ref):
    n_core = own_ref.shape[1]
    width = kernel_ref.shape[1]
    rows = 16
    row = jnp.broadcast_to(kernel_ref[...], (rows, width))
    first = pltpu.roll(row, 0, 1, stride=1, stride_axis=0)
    for g in range(BLOCK // rows):
        part = first if g == 0 else pltpu.roll(first, g * rows, 1)
        strip_ref[g * rows : (g + 1) * rows, :] = part[:, BLOCK:].astype(BF16)
    own = own_ref[...]
    for b, field in enumerate(toeplitz(own, strip_ref, 0, n_core // BLOCK)):
        here = slice(b * BLOCK, (b + 1) * BLOCK)
        base_ref[:, here] = right_ref[:, here].astype(F32) - own[:, here].astype(F32) - field
    member_ref[...] = one_hot(labels_ref[...], member_ref.shape[0])


def clear_kernel(_, columns_ref):
    columns_ref[...] = jnp.zeros_like(columns_ref)


def columns_kernel(_, *refs):
    parts, columns_ref = refs[:-1], refs[-1]
    n_dev = len(parts)
    targets = partners("col")
    half = parts[0].shape[0] // len(targets)
    dev = lax.axis_index("dev")
    for d, by in enumerate(targets):
        source = pl.multiple_of(by * half, half)
        for e in range(n_dev):
            target = pl.multiple_of(lax.rem(dev + e, n_dev) * half, half)
            columns_ref[d, pl.ds(target, half), :] = parts[e][pl.ds(source, half), :]


def residual_kernel(unknowns, base_ref, to, ti, uo, ui, strip_ref, inv_ref, member_ref, ro, rx, ri, res_ref):
    n_core = base_ref.shape[1]
    rows, shell = to.shape
    odd_row, odd_col = place("row")[1] == 1, place("col")[1] == 1
    low = [jnp.where(odd_row, ti[...], to[...]), jnp.where(odd_row, to[...], ti[...])]
    high = [jnp.where(odd_col, ui[...], uo[...]), jnp.where(odd_col, uo[...], ui[...])]
    shells = jnp.concatenate(low + high, axis=1)
    for b in range(n_core // BLOCK):
        start = 2 * n_core - BLOCK - BLOCK * b
        here = slice(b * BLOCK, (b + 1) * BLOCK)
        field = mm_nt(shells, strip_ref[:, start : start + shells.shape[1]])
        res_ref[:, here] = (base_ref[:, here] - field).astype(BF16)
    res = res_ref[...]
    coarse = mm_nt(res, member_ref[:unknowns, :]).astype(BF16)
    for out in (ro, rx, ri):
        out[-rows:, :] = jnp.zeros((rows, LANES), BF16)
        out[-rows:, :unknowns] = coarse
    back = mm(res, inv_ref[:, n_core : n_core + 2 * shell]).astype(BF16)
    ro[:rows, :] = jnp.where(odd_row, back[:, shell:], back[:, :shell])
    ri[:rows, :] = jnp.where(odd_row, back[:, :shell], back[:, shell:])


def outer_kernel(res_ref, inv_ref, co, ci):
    shell = co.shape[1]
    odd_col = place("col")[1] == 1
    back = mm(res_ref[...], inv_ref[:, -2 * shell :]).astype(BF16)
    co[...] = jnp.where(odd_col, back[:, shell:], back[:, :shell])
    ci[...] = jnp.where(odd_col, back[:, :shell], back[:, shell:])


def partial_kernel(columns_ref, co, ci, *refs):
    sources = partners("row")
    n_bx = len(sources)
    gathered, outs = refs[:n_bx], refs[n_bx:]
    width = columns_ref.shape[2]
    rows = co.shape[0]
    total = jnp.zeros((rows, width), F32)
    for bx, ref in zip(sources, gathered):
        piece = ref[-rows:, :].astype(F32)
        if width > LANES:
            piece = jnp.concatenate([piece, jnp.zeros((rows, width - LANES), F32)], axis=1)
        total = total + pltpu.roll(piece, bx * (width // n_bx), 1)
    total = total.astype(BF16)
    outs[1][:rows, :] = co[...].astype(F32)
    outs[2][:rows, :] = ci[...].astype(F32)
    for d, out in enumerate(outs):
        out[-rows:, :] = mm_nt(total, columns_ref[d])


def local_kernel(res_ref, inv_ref, spots_ref, ro, ri, acc_ref):
    rows, n_core = res_ref.shape
    arrived = jnp.concatenate([ro[:rows, :], ri[:rows, :]], axis=1)
    added = mm_nt(arrived, spots_ref[:, : arrived.shape[1]])
    acc_ref[...] = mm(res_ref[...], inv_ref[:, :n_core]).astype(BF16).astype(F32) + added


def final_kernel(acc_ref, member_ref, spots_ref, *refs):
    parts, out_ref = refs[:-1], refs[-1]
    rows = acc_ref.shape[0]
    solved = parts[0][...]
    for part in parts[1:]:
        solved = solved + part[-rows:, :]
    high = solved.astype(BF16)
    low = (solved - high.astype(F32)).astype(BF16)
    both = mm(jnp.concatenate([high, low], axis=0), member_ref[...])
    arrived = jnp.concatenate([parts[1][:rows, :], parts[2][:rows, :]], axis=1).astype(BF16)
    added = mm_nt(arrived, spots_ref[:, arrived.shape[1] :])
    out_ref[...] = (acc_ref[...] + added + both[:rows] + both[rows:]).astype(BF16)


def call(body, shapes, *args, hbm=(), scratch=(), aliases={}, limit=16, flops=10**6):
    out_shape = [jax.ShapeDtypeStruct(s, t) for s, t in shapes]
    args = [pltpu.with_memory_space_constraint(a, pltpu.HBM) if i in hbm else a for i, a in enumerate(args)]
    size = sum(a.size * a.dtype.itemsize for a in args)
    return pl.pallas_call(
        body,
        out_shape=out_shape,
        in_specs=[HBM if i in hbm else VMEM for i in range(len(args))],
        out_specs=[VMEM] * len(out_shape),
        scratch_shapes=scratch,
        input_output_aliases=aliases,
        compiler_params=pltpu.CompilerParams(vmem_limit_bytes=limit << 20),
        cost_estimate=pl.CostEstimate(flops=flops, bytes_accessed=size, transcendentals=0),
    )(*args)


def per_device(iterate, right_side, kernel, inverse_rows, coarse_inverse, aggregate, send_index):
    own = iterate[:, 0, 0, :]
    right = right_side[:, 0, 0, :]
    inverse = inverse_rows[0, 0]
    labels = aggregate[0]
    send = send_index[0, 0]
    mine = coarse_inverse.T
    rows, n_core = own.shape
    n_shell = send.shape[1]
    n_patch = inverse.shape[1]
    n_bx, n_by, n_dev = (lax.axis_size(a) for a in ("row", "col", "dev"))
    coarse_rows = coarse_inverse.shape[0]
    shell = ((rows, n_shell), BF16)
    double = ((2 * rows, LANES), BF16)

    held = (own, right, labels, mine, kernel)
    co, ro, ci, ri, spots, own, right, labels, mine, kernel = call(
        gather_kernel,
        [shell] * 4 + [((n_core, 4 * n_shell), BF16)] + [(a.shape, a.dtype) for a in held],
        send,
        *held,
        hbm=range(6),
        scratch=[pltpu.VMEM(send.shape, send.dtype), pltpu.SemaphoreType.DMA((6,))],
    )
    column_shape = ((n_by, LANES, coarse_rows), BF16)
    (cleared,) = call(clear_kernel, [column_shape], co, flops=8 * 10**9)
    uo = lax.ppermute(co, "col", outer_pairs(n_by))
    to = lax.ppermute(ro, "row", outer_pairs(n_bx))
    ui = lax.ppermute(ci, "col", inner_pairs(n_by))
    ti = lax.ppermute(ri, "row", inner_pairs(n_bx))
    halves = [mine] + [lax.ppermute(mine, "dev", shifted(n_dev, -e)) for e in range(1, n_dev)]

    width = n_core + n_patch
    padded = jnp.pad(kernel.astype(F32), (1, width - kernel.shape[0] - 1))[None, :]
    strip, base, member = call(
        strip_kernel,
        [((BLOCK, width - BLOCK), BF16), ((rows, n_core), F32), ((LANES, n_core), BF16)],
        padded,
        own,
        right,
        labels,
    )
    unknowns = coarse_rows // n_bx
    ro, rx, ri, res = call(
        functools.partial(residual_kernel, unknowns),
        [double, shell, double, ((rows, n_core), BF16)],
        base,
        to,
        ti,
        uo,
        ui,
        strip,
        inverse,
        member,
    )
    ao = lax.ppermute(ro, "row", outer_pairs(n_bx))
    rest = [lax.ppermute(rx, "row", shifted(n_bx, -o)) for o in range(2, n_bx - 1)]
    ai = lax.ppermute(ri, "row", inner_pairs(n_bx))
    co, ci = call(outer_kernel, [shell, shell], res, inverse)
    (columns,) = call(columns_kernel, [column_shape], cleared, *halves, aliases={0: 0})
    single, wide = ((rows, LANES), F32), ((2 * rows, LANES), F32)
    partials = call(partial_kernel, [single, wide, wide] + [single] * (n_by - 3), columns, co, ci, rx, ao, ai, *rest)
    so = lax.ppermute(partials[1], "col", outer_pairs(n_by))
    others = [lax.ppermute(partials[d + 1], "col", shifted(n_by, d)) for d in range(2, n_by - 1)]
    si = lax.ppermute(partials[2], "col", inner_pairs(n_by))
    (acc,) = call(local_kernel, [((rows, n_core), F32)], res, inverse, spots, ao, ai)
    (out,) = call(final_kernel, [((rows, n_core), BF16)], acc, member, spots, partials[0], so, si, *others)
    return out[:, None, None, :]


def solution(mesh):
    in_specs = (
        P("dev", "row", "col", None),
        P("dev", "row", "col", None),
        P(),
        P("row", "col", None, None),
        P("col", ("row", "dev")),
        P("row", "col", None),
        P("row", "col", None, None),
    )
    out_specs = P("dev", "row", "col", None)

    return jax.shard_map(per_device, mesh=mesh, in_specs=in_specs, out_specs=out_specs, check_vma=False)
```

```python
import functools

import jax
import jax.numpy as jnp
from jax import lax
from jax.experimental import pallas as pl
from jax.experimental.pallas import tpu as pltpu
from jax.sharding import PartitionSpec as P


LANES = 128
BLOCK = 256
VMEM = pl.BlockSpec(memory_space=pltpu.VMEM)
HBM = pl.BlockSpec(memory_space=pltpu.HBM)
F32 = jnp.float32
BF16 = jnp.bfloat16


def mm(left, right):
    return jnp.dot(left, right, preferred_element_type=F32)


def mm_nt(left, right):
    return lax.dot_general(left, right, (((1,), (1,)), ((), ())), preferred_element_type=F32)


def one_hot(labels, rows):
    shape = (rows, labels.shape[1])
    hit = lax.broadcasted_iota(jnp.int16, shape, 0) == jnp.broadcast_to(labels.astype(jnp.int16), shape)
    return jnp.where(hit, jnp.ones(shape, BF16), jnp.zeros(shape, BF16))


def toeplitz(values, strip_ref, offset, blocks):
    rows, parts = values.shape[0], values.shape[1] // BLOCK
    stacked = jnp.concatenate([values[:, u * BLOCK : (u + 1) * BLOCK] for u in range(parts)], axis=0)
    starts = [offset + BLOCK * t for t in range(blocks - 1 + parts)]
    tiles = [mm_nt(stacked, strip_ref[:, start : start + BLOCK]) for start in starts]
    return [
        sum(tiles[blocks - 1 - b + u][u * rows : (u + 1) * rows] for u in range(parts)) for b in range(blocks)
    ]


def place(axis):
    index = lax.axis_index(axis)
    return index, lax.rem(index, 2), lax.axis_size(axis)


def partners(axis):
    index, odd, count = place(axis)
    outer = lax.rem(index + jnp.where(odd == 1, 1, count - 1), count)
    inner = index + jnp.where(odd == 1, -1, 1)
    return [index, outer, inner] + [lax.rem(index + o, count) for o in range(2, count - 1)]


def outer_pairs(count):
    return [(i, (i + 1) % count if i % 2 else (i - 1) % count) for i in range(count)]


def inner_pairs(count):
    return [(i, i ^ 1) for i in range(count)]


def shifted(count, step):
    return [(i, (i + step) % count) for i in range(count)]


def gather_kernel(send_hbm, own_hbm, *refs):
    rest = (len(refs) - 8) // 2
    more_hbm, (co, ro, ci, ri, spots_ref, own_ref) = refs[:rest], refs[rest : rest + 6]
    more, (send_ref, sems) = refs[rest + 6 : -2], refs[-2:]
    pairs = zip((send_hbm, own_hbm, *more_hbm), (send_ref, own_ref, *more))
    copies = [pltpu.make_async_copy(a, b, sems.at[i]) for i, (a, b) in enumerate(pairs)]
    for copy in copies:
        copy.start()
    copies[0].wait()
    n_core = own_ref.shape[1]
    shell = send_ref.shape[1]
    hots = []
    for slot, (axis, base, inner) in enumerate((("row", 0, 0), ("row", 0, 1), ("col", 2, 0), ("col", 2, 1))):
        odd = place(axis)[1]
        direction = base + jnp.where(odd == 1, inner, 1 - inner)
        hot = one_hot(send_ref[pl.ds(direction, 1), :], n_core)
        spots_ref[:, slot * shell : (slot + 1) * shell] = hot
        hots.append(hot)
    copies[1].wait()
    own = own_ref[...]
    for slot, out in ((2, co), (0, ro), (3, ci), (1, ri)):
        out[...] = mm(own, spots_ref[:, slot * shell : (slot + 1) * shell]).astype(BF16)
    for copy in copies[2:]:
        copy.wait()


def build_strip(kernel_ref, own_ref, right_ref, labels_ref, strip_ref, base_ref, member_ref):
    n_core = own_ref.shape[1]
    width = kernel_ref.shape[1]
    rows = 16
    row = jnp.broadcast_to(kernel_ref[...], (rows, width))
    first = pltpu.roll(row, 0, 1, stride=1, stride_axis=0)
    for g in range(BLOCK // rows):
        part = first if g == 0 else pltpu.roll(first, g * rows, 1)
        strip_ref[g * rows : (g + 1) * rows, :] = part[:, BLOCK:].astype(BF16)
    own = own_ref[...]
    for b, field in enumerate(toeplitz(own, strip_ref, 0, n_core // BLOCK)):
        here = slice(b * BLOCK, (b + 1) * BLOCK)
        base_ref[:, here] = right_ref[:, here].astype(F32) - own[:, here].astype(F32) - field
    member_ref[...] = one_hot(labels_ref[...], member_ref.shape[0])


def is_early():
    index, _, count = place("dev")
    return index < count - 1


def early_kernel(*refs):
    @pl.when(is_early())
    def _():
        build_strip(*refs)


def late_kernel(*refs):
    @pl.when(jnp.logical_not(is_early()))
    def _():
        build_strip(*refs[:4], *refs[-3:])


def clear_kernel(_, columns_ref):
    columns_ref[...] = jnp.zeros_like(columns_ref)


def columns_kernel(_, *refs):
    parts, columns_ref = refs[:-1], refs[-1]
    n_dev = len(parts)
    targets = partners("col")
    half = parts[0].shape[0] // len(targets)
    dev = lax.axis_index("dev")
    for d, by in enumerate(targets):
        source = pl.multiple_of(by * half, half)
        for e in range(n_dev):
            target = pl.multiple_of(lax.rem(dev + e, n_dev) * half, half)
            columns_ref[d, pl.ds(target, half), :] = parts[e][pl.ds(source, half), :]


def residual_kernel(unknowns, base_ref, to, ti, uo, ui, strip_ref, inv_ref, member_ref, ro, rx, ri, res_ref):
    n_core = base_ref.shape[1]
    rows, shell = to.shape
    odd_row, odd_col = place("row")[1] == 1, place("col")[1] == 1
    low = [jnp.where(odd_row, ti[...], to[...]), jnp.where(odd_row, to[...], ti[...])]
    high = [jnp.where(odd_col, ui[...], uo[...]), jnp.where(odd_col, uo[...], ui[...])]
    shells = jnp.concatenate(low + high, axis=1)
    for b in range(n_core // BLOCK):
        start = 2 * n_core - BLOCK - BLOCK * b
        here = slice(b * BLOCK, (b + 1) * BLOCK)
        field = mm_nt(shells, strip_ref[:, start : start + shells.shape[1]])
        res_ref[:, here] = (base_ref[:, here] - field).astype(BF16)
    res = res_ref[...]
    coarse = mm_nt(res, member_ref[:unknowns, :]).astype(BF16)
    for out in (ro, rx, ri):
        out[-rows:, :] = jnp.zeros((rows, LANES), BF16)
        out[-rows:, :unknowns] = coarse
    back = mm(res, inv_ref[:, n_core : n_core + 2 * shell]).astype(BF16)
    ro[:rows, :] = jnp.where(odd_row, back[:, shell:], back[:, :shell])
    ri[:rows, :] = jnp.where(odd_row, back[:, :shell], back[:, shell:])


def outer_kernel(res_ref, inv_ref, co, ci):
    shell = co.shape[1]
    odd_col = place("col")[1] == 1
    back = mm(res_ref[...], inv_ref[:, -2 * shell :]).astype(BF16)
    co[...] = jnp.where(odd_col, back[:, shell:], back[:, :shell])
    ci[...] = jnp.where(odd_col, back[:, :shell], back[:, shell:])


def partial_kernel(unknowns, columns_ref, co, ci, *refs):
    sources = partners("row")
    n_bx = len(sources)
    gathered, outs = refs[:n_bx], refs[n_bx:]
    width = columns_ref.shape[2]
    rows = co.shape[0]
    total = jnp.zeros((rows, width), F32)
    for bx, ref in zip(sources, gathered):
        piece = ref[-rows:, :].astype(F32)
        if width > LANES:
            piece = jnp.concatenate([piece, jnp.zeros((rows, width - LANES), F32)], axis=1)
        total = total + pltpu.roll(piece, bx * (width // n_bx), 1)
    total = total.astype(BF16)
    outs[1][:rows, :] = co[...]
    outs[2][:rows, :] = ci[...]
    height = outs[0].shape[0]
    for d, out in enumerate(outs):
        part = pack(mm_nt(total, columns_ref[d]), unknowns)
        if d == 0:
            out[...] = part
        else:
            high = part.astype(BF16)
            out[-2 * height : -height, :] = high
            out[-height:, :] = (part - high.astype(F32)).astype(BF16)


def local_kernel(res_ref, inv_ref, spots_ref, ro, ri, acc_ref):
    rows, n_core = res_ref.shape
    arrived = jnp.concatenate([ro[:rows, :], ri[:rows, :]], axis=1)
    added = mm_nt(arrived, spots_ref[:, : arrived.shape[1]])
    acc_ref[...] = mm(res_ref[...], inv_ref[:, :n_core]).astype(BF16).astype(F32) + added


def final_kernel(unknowns, acc_ref, member_ref, spots_ref, *refs):
    parts, out_ref = refs[:-1], refs[-1]
    rows = acc_ref.shape[0]
    height = parts[0].shape[0]
    solved = parts[0][...]
    for part in parts[1:]:
        solved = solved + part[-2 * height : -height, :].astype(F32) + part[-height:, :].astype(F32)
    solved = unpack(solved, unknowns)
    high = solved.astype(BF16)
    low = (solved - high.astype(F32)).astype(BF16)
    both = mm(jnp.concatenate([high, low], axis=0), member_ref[...])
    arrived = jnp.concatenate([parts[1][:rows, :], parts[2][:rows, :]], axis=1)
    added = mm_nt(arrived, spots_ref[:, arrived.shape[1] :])
    out_ref[...] = (acc_ref[...] + added + both[:rows] + both[rows:]).astype(BF16)


def pack(value, unknowns):
    groups = LANES // unknowns
    height = value.shape[0] // groups
    parts = [pltpu.roll(value[q * height : (q + 1) * height, :], q * unknowns, 1) for q in range(1, groups)]
    return sum(parts, value[:height, :])


def unpack(packed, unknowns):
    keep = lax.broadcasted_iota(jnp.int32, packed.shape, 1) < unknowns
    parts = [packed] + [pltpu.roll(packed, LANES - q * unknowns, 1) for q in range(1, LANES // unknowns)]
    return jnp.concatenate([jnp.where(keep, part, 0.0) for part in parts], axis=0)


def call(body, shapes, *args, hbm=(), scratch=(), aliases={}, limit=16, flops=10**6):
    out_shape = [jax.ShapeDtypeStruct(s, t) for s, t in shapes]
    args = [pltpu.with_memory_space_constraint(a, pltpu.HBM) if i in hbm else a for i, a in enumerate(args)]
    size = sum(a.size * a.dtype.itemsize for a in args)
    return pl.pallas_call(
        body,
        out_shape=out_shape,
        in_specs=[HBM if i in hbm else VMEM for i in range(len(args))],
        out_specs=[VMEM] * len(out_shape),
        scratch_shapes=scratch,
        input_output_aliases=aliases,
        compiler_params=pltpu.CompilerParams(vmem_limit_bytes=limit << 20),
        cost_estimate=pl.CostEstimate(flops=flops, bytes_accessed=size, transcendentals=0),
    )(*args)


def per_device(iterate, right_side, kernel, inverse_rows, coarse_inverse, aggregate, send_index):
    own = iterate[:, 0, 0, :]
    right = right_side[:, 0, 0, :]
    inverse = inverse_rows[0, 0]
    labels = aggregate[0]
    send = send_index[0, 0]
    mine = coarse_inverse.T
    rows, n_core = own.shape
    n_shell = send.shape[1]
    n_patch = inverse.shape[1]
    n_bx, n_by, n_dev = (lax.axis_size(a) for a in ("row", "col", "dev"))
    coarse_rows = coarse_inverse.shape[0]
    shell = ((rows, n_shell), BF16)
    double = ((2 * rows, LANES), BF16)

    held = (own, right, labels, mine, kernel)
    co, ro, ci, ri, spots, own, right, labels, mine, kernel = call(
        gather_kernel,
        [shell] * 4 + [((n_core, 4 * n_shell), BF16)] + [(a.shape, a.dtype) for a in held],
        send,
        *held,
        hbm=range(6),
        scratch=[pltpu.VMEM(send.shape, send.dtype), pltpu.SemaphoreType.DMA((6,))],
    )
    column_shape = ((n_by, LANES, coarse_rows), BF16)
    (cleared,) = call(clear_kernel, [column_shape], co, flops=8 * 10**9)
    uo = lax.ppermute(co, "col", outer_pairs(n_by))
    to = lax.ppermute(ro, "row", outer_pairs(n_bx))
    ui = lax.ppermute(ci, "col", inner_pairs(n_by))
    ti = lax.ppermute(ri, "row", inner_pairs(n_bx))
    halves = [mine] + [lax.ppermute(mine, "dev", shifted(n_dev, -e)) for e in range(1, n_dev)]

    width = n_core + n_patch
    padded = jnp.pad(kernel.astype(F32), (1, width - kernel.shape[0] - 1))[None, :]
    inputs = (padded, own, right, labels)
    shapes = [((BLOCK, width - BLOCK), BF16), ((rows, n_core), F32), ((LANES, n_core), BF16)]
    built = call(early_kernel, shapes, *inputs)
    strip_aliases = {len(inputs) + i: i for i in range(3)}
    strip, base, member = call(late_kernel, shapes, *inputs, *built, aliases=strip_aliases)
    unknowns = coarse_rows // n_bx
    ro, rx, ri, res = call(
        functools.partial(residual_kernel, unknowns),
        [double, shell, double, ((rows, n_core), BF16)],
        base,
        to,
        ti,
        uo,
        ui,
        strip,
        inverse,
        member,
    )
    ao = lax.ppermute(ro, "row", outer_pairs(n_bx))
    rest = [lax.ppermute(rx, "row", shifted(n_bx, -o)) for o in range(2, n_bx - 1)]
    ai = lax.ppermute(ri, "row", inner_pairs(n_bx))
    co, ci = call(outer_kernel, [shell, shell], res, inverse)
    (columns,) = call(columns_kernel, [column_shape], cleared, *halves, aliases={0: 0})
    height = rows * unknowns // LANES
    single, wide = ((2 * height, LANES), BF16), ((rows + 2 * height, LANES), BF16)
    partials = call(
        functools.partial(partial_kernel, unknowns),
        [((height, LANES), F32), wide, wide] + [single] * (n_by - 3),
        columns,
        co,
        ci,
        rx,
        ao,
        ai,
        *rest,
    )
    so = lax.ppermute(partials[1], "col", outer_pairs(n_by))
    others = [lax.ppermute(partials[d + 1], "col", shifted(n_by, d)) for d in range(2, n_by - 1)]
    si = lax.ppermute(partials[2], "col", inner_pairs(n_by))
    (acc,) = call(local_kernel, [((rows, n_core), F32)], res, inverse, spots, ao, ai)
    (out,) = call(functools.partial(final_kernel, unknowns), [((rows, n_core), BF16)], acc, member, spots, partials[0], so, si, *others)
    return out[:, None, None, :]


def solution(mesh):
    in_specs = (
        P("dev", "row", "col", None),
        P("dev", "row", "col", None),
        P(),
        P("row", "col", None, None),
        P("col", ("row", "dev")),
        P("row", "col", None),
        P("row", "col", None, None),
    )
    out_specs = P("dev", "row", "col", None)

    return jax.shard_map(per_device, mesh=mesh, in_specs=in_specs, out_specs=out_specs, check_vma=False)
```

```python
import functools

import jax
import jax.numpy as jnp
from jax import lax
from jax.experimental import pallas as pl
from jax.experimental.pallas import tpu as pltpu
from jax.sharding import PartitionSpec as P


LANES = 128
BLOCK = 256
VMEM = pl.BlockSpec(memory_space=pltpu.VMEM)
HBM = pl.BlockSpec(memory_space=pltpu.HBM)
F32 = jnp.float32
BF16 = jnp.bfloat16


def mm(left, right):
    return jnp.dot(left, right, preferred_element_type=F32)


def mm_nt(left, right):
    return lax.dot_general(left, right, (((1,), (1,)), ((), ())), preferred_element_type=F32)


def one_hot(labels, rows):
    shape = (rows, labels.shape[1])
    hit = lax.broadcasted_iota(jnp.int16, shape, 0) == jnp.broadcast_to(labels.astype(jnp.int16), shape)
    return jnp.where(hit, jnp.ones(shape, BF16), jnp.zeros(shape, BF16))


def toeplitz(values, strip_ref, offset, blocks):
    rows, parts = values.shape[0], values.shape[1] // BLOCK
    stacked = jnp.concatenate([values[:, u * BLOCK : (u + 1) * BLOCK] for u in range(parts)], axis=0)
    starts = [offset + BLOCK * t for t in range(blocks - 1 + parts)]
    tiles = [mm_nt(stacked, strip_ref[:, start : start + BLOCK]) for start in starts]
    return [
        sum(tiles[blocks - 1 - b + u][u * rows : (u + 1) * rows] for u in range(parts)) for b in range(blocks)
    ]


def place(axis):
    index = lax.axis_index(axis)
    return index, lax.rem(index, 2), lax.axis_size(axis)


def partners(axis):
    index, odd, count = place(axis)
    outer = lax.rem(index + jnp.where(odd == 1, 1, count - 1), count)
    inner = index + jnp.where(odd == 1, -1, 1)
    return [index, outer, inner] + [lax.rem(index + o, count) for o in range(2, count - 1)]


def outer_pairs(count):
    return [(i, (i + 1) % count if i % 2 else (i - 1) % count) for i in range(count)]


def inner_pairs(count):
    return [(i, i ^ 1) for i in range(count)]


def shifted(count, step):
    return [(i, (i + step) % count) for i in range(count)]


def gather_kernel(send_hbm, own_hbm, *refs):
    rest = (len(refs) - 8) // 2
    more_hbm, (co, ro, ci, ri, spots_ref, own_ref) = refs[:rest], refs[rest : rest + 6]
    more, (send_ref, sems) = refs[rest + 6 : -2], refs[-2:]
    pairs = zip((send_hbm, own_hbm, *more_hbm), (send_ref, own_ref, *more))
    copies = [pltpu.make_async_copy(a, b, sems.at[i]) for i, (a, b) in enumerate(pairs)]
    for copy in copies:
        copy.start()
    copies[0].wait()
    n_core = own_ref.shape[1]
    shell = send_ref.shape[1]
    labels = []
    for axis, base in (("row", 0), ("col", 2)):
        odd = place(axis)[1]
        labels += [send_ref[pl.ds(base + 1 - odd, 1), :], send_ref[pl.ds(base + odd, 1), :]]
    for slot, label in enumerate(labels):
        spots_ref[:, slot * shell : (slot + 1) * shell] = one_hot(label, n_core)
    copies[1].wait()
    sent = mm(own_ref[...], spots_ref[...]).astype(BF16)
    for slot, out in enumerate((ro, ri, co, ci)):
        out[...] = sent[:, slot * shell : (slot + 1) * shell]
    for copy in copies[2:]:
        copy.wait()


def build_strip(kernel_ref, own_ref, right_ref, labels_ref, strip_ref, base_ref, member_ref):
    n_core = own_ref.shape[1]
    width = kernel_ref.shape[1]
    rows = 16
    row = jnp.broadcast_to(kernel_ref[...], (rows, width))
    first = pltpu.roll(row, 0, 1, stride=1, stride_axis=0)
    for g in range(BLOCK // rows):
        part = first if g == 0 else pltpu.roll(first, g * rows, 1)
        strip_ref[g * rows : (g + 1) * rows, :] = part[:, BLOCK:].astype(BF16)
    own = own_ref[...]
    for b, field in enumerate(toeplitz(own, strip_ref, 0, n_core // BLOCK)):
        here = slice(b * BLOCK, (b + 1) * BLOCK)
        base_ref[:, here] = right_ref[:, here].astype(F32) - own[:, here].astype(F32) - field
    member_ref[...] = one_hot(labels_ref[...], member_ref.shape[0])


def is_early():
    index, _, count = place("dev")
    return index < count - 1


def early_kernel(*refs):
    @pl.when(is_early())
    def _():
        build_strip(*refs)


def late_kernel(*refs):
    @pl.when(jnp.logical_not(is_early()))
    def _():
        build_strip(*refs[:4], *refs[-3:])


def clear_kernel(_, columns_ref):
    columns_ref[...] = jnp.zeros_like(columns_ref)


def columns_kernel(_, *refs):
    parts, columns_ref = refs[:-1], refs[-1]
    n_dev = len(parts)
    targets = partners("col")
    half = parts[0].shape[0] // len(targets)
    dev = lax.axis_index("dev")
    for d, by in enumerate(targets):
        source = pl.multiple_of(by * half, half)
        for e in range(n_dev):
            target = pl.multiple_of(lax.rem(dev + e, n_dev) * half, half)
            columns_ref[d, pl.ds(target, half), :] = parts[e][pl.ds(source, half), :]


def residual_kernel(unknowns, base_ref, to, ti, uo, ui, strip_ref, inv_ref, member_ref, ro, rx, ri, res_ref):
    n_core = base_ref.shape[1]
    rows, shell = to.shape
    odd_row, odd_col = place("row")[1] == 1, place("col")[1] == 1
    low = [jnp.where(odd_row, ti[...], to[...]), jnp.where(odd_row, to[...], ti[...])]
    high = [jnp.where(odd_col, ui[...], uo[...]), jnp.where(odd_col, uo[...], ui[...])]
    shells = jnp.concatenate(low + high, axis=1)
    for b in range(n_core // BLOCK):
        start = 2 * n_core - BLOCK - BLOCK * b
        here = slice(b * BLOCK, (b + 1) * BLOCK)
        field = mm_nt(shells, strip_ref[:, start : start + shells.shape[1]])
        res_ref[:, here] = (base_ref[:, here] - field).astype(BF16)
    res = res_ref[...]
    coarse = mm_nt(res, member_ref[:unknowns, :]).astype(BF16)
    for out in (ro, rx, ri):
        out[-rows:, :] = jnp.zeros((rows, LANES), BF16)
        out[-rows:, :unknowns] = coarse
    back = mm(res, inv_ref[:, n_core : n_core + 2 * shell]).astype(BF16)
    ro[:rows, :] = jnp.where(odd_row, back[:, shell:], back[:, :shell])
    ri[:rows, :] = jnp.where(odd_row, back[:, :shell], back[:, shell:])


def outer_kernel(res_ref, inv_ref, co, ci):
    shell = co.shape[1]
    odd_col = place("col")[1] == 1
    back = mm(res_ref[...], inv_ref[:, -2 * shell :]).astype(BF16)
    co[...] = jnp.where(odd_col, back[:, shell:], back[:, :shell])
    ci[...] = jnp.where(odd_col, back[:, :shell], back[:, shell:])


def partial_kernel(unknowns, columns_ref, co, ci, *refs):
    sources = partners("row")
    n_bx = len(sources)
    gathered, outs = refs[:n_bx], refs[n_bx:]
    width = columns_ref.shape[2]
    rows = co.shape[0]
    total = jnp.zeros((rows, width), F32)
    for bx, ref in zip(sources, gathered):
        piece = ref[-rows:, :].astype(F32)
        if width > LANES:
            piece = jnp.concatenate([piece, jnp.zeros((rows, width - LANES), F32)], axis=1)
        total = total + pltpu.roll(piece, bx * (width // n_bx), 1)
    total = total.astype(BF16)
    outs[1][:rows, :] = co[...]
    outs[2][:rows, :] = ci[...]
    height = outs[0].shape[0]
    for d, out in enumerate(outs):
        part = pack(mm_nt(total, columns_ref[d]), unknowns)
        if d == 0:
            out[...] = part
        else:
            high = part.astype(BF16)
            out[-2 * height : -height, :] = high
            out[-height:, :] = (part - high.astype(F32)).astype(BF16)


def local_kernel(res_ref, inv_ref, spots_ref, ro, ri, acc_ref):
    rows, n_core = res_ref.shape
    arrived = jnp.concatenate([ro[:rows, :], ri[:rows, :]], axis=1)
    added = mm_nt(arrived, spots_ref[:, : arrived.shape[1]])
    acc_ref[...] = mm(res_ref[...], inv_ref[:, :n_core]).astype(BF16).astype(F32) + added


def final_kernel(unknowns, acc_ref, member_ref, spots_ref, *refs):
    parts, out_ref = refs[:-1], refs[-1]
    rows = acc_ref.shape[0]
    height = parts[0].shape[0]
    solved = parts[0][...]
    for part in parts[1:]:
        solved = solved + part[-2 * height : -height, :].astype(F32) + part[-height:, :].astype(F32)
    solved = unpack(solved, unknowns)
    high = solved.astype(BF16)
    low = (solved - high.astype(F32)).astype(BF16)
    both = mm(jnp.concatenate([high, low], axis=0), member_ref[...])
    arrived = jnp.concatenate([parts[1][:rows, :], parts[2][:rows, :]], axis=1)
    added = mm_nt(arrived, spots_ref[:, arrived.shape[1] :])
    out_ref[...] = (acc_ref[...] + added + both[:rows] + both[rows:]).astype(BF16)


def pack(value, unknowns):
    groups = LANES // unknowns
    height = value.shape[0] // groups
    parts = [pltpu.roll(value[q * height : (q + 1) * height, :], q * unknowns, 1) for q in range(1, groups)]
    return sum(parts, value[:height, :])


def unpack(packed, unknowns):
    keep = lax.broadcasted_iota(jnp.int32, packed.shape, 1) < unknowns
    parts = [packed] + [pltpu.roll(packed, LANES - q * unknowns, 1) for q in range(1, LANES // unknowns)]
    return jnp.concatenate([jnp.where(keep, part, 0.0) for part in parts], axis=0)


def call(body, shapes, *args, hbm=(), scratch=(), aliases={}, limit=16, flops=10**6):
    out_shape = [jax.ShapeDtypeStruct(s, t) for s, t in shapes]
    args = [pltpu.with_memory_space_constraint(a, pltpu.HBM) if i in hbm else a for i, a in enumerate(args)]
    size = sum(a.size * a.dtype.itemsize for a in args)
    return pl.pallas_call(
        body,
        out_shape=out_shape,
        in_specs=[HBM if i in hbm else VMEM for i in range(len(args))],
        out_specs=[VMEM] * len(out_shape),
        scratch_shapes=scratch,
        input_output_aliases=aliases,
        compiler_params=pltpu.CompilerParams(vmem_limit_bytes=limit << 20),
        cost_estimate=pl.CostEstimate(flops=flops, bytes_accessed=size, transcendentals=0),
    )(*args)


def per_device(iterate, right_side, kernel, inverse_rows, coarse_inverse, aggregate, send_index):
    own = iterate[:, 0, 0, :]
    right = right_side[:, 0, 0, :]
    inverse = inverse_rows[0, 0]
    labels = aggregate[0]
    send = send_index[0, 0]
    mine = coarse_inverse.T
    rows, n_core = own.shape
    n_shell = send.shape[1]
    n_patch = inverse.shape[1]
    n_bx, n_by, n_dev = (lax.axis_size(a) for a in ("row", "col", "dev"))
    coarse_rows = coarse_inverse.shape[0]
    shell = ((rows, n_shell), BF16)
    double = ((2 * rows, LANES), BF16)

    held = (own, right, labels, mine, kernel)
    co, ro, ci, ri, spots, own, right, labels, mine, kernel = call(
        gather_kernel,
        [shell] * 4 + [((n_core, 4 * n_shell), BF16)] + [(a.shape, a.dtype) for a in held],
        send,
        *held,
        hbm=range(6),
        scratch=[pltpu.VMEM(send.shape, send.dtype), pltpu.SemaphoreType.DMA((6,))],
    )
    column_shape = ((n_by, LANES, coarse_rows), BF16)
    (cleared,) = call(clear_kernel, [column_shape], co, flops=8 * 10**9)
    uo = lax.ppermute(co, "col", outer_pairs(n_by))
    to = lax.ppermute(ro, "row", outer_pairs(n_bx))
    ui = lax.ppermute(ci, "col", inner_pairs(n_by))
    ti = lax.ppermute(ri, "row", inner_pairs(n_bx))
    halves = [mine] + [lax.ppermute(mine, "dev", shifted(n_dev, -e)) for e in range(1, n_dev)]

    width = n_core + n_patch
    padded = jnp.pad(kernel.astype(F32), (1, width - kernel.shape[0] - 1))[None, :]
    inputs = (padded, own, right, labels)
    shapes = [((BLOCK, width - BLOCK), BF16), ((rows, n_core), F32), ((LANES, n_core), BF16)]
    built = call(early_kernel, shapes, *inputs)
    strip_aliases = {len(inputs) + i: i for i in range(3)}
    strip, base, member = call(late_kernel, shapes, *inputs, *built, aliases=strip_aliases)
    unknowns = coarse_rows // n_bx
    ro, rx, ri, res = call(
        functools.partial(residual_kernel, unknowns),
        [double, shell, double, ((rows, n_core), BF16)],
        base,
        to,
        ti,
        uo,
        ui,
        strip,
        inverse,
        member,
    )
    ao = lax.ppermute(ro, "row", outer_pairs(n_bx))
    rest = [lax.ppermute(rx, "row", shifted(n_bx, -o)) for o in range(2, n_bx - 1)]
    ai = lax.ppermute(ri, "row", inner_pairs(n_bx))
    co, ci = call(outer_kernel, [shell, shell], res, inverse)
    (columns,) = call(columns_kernel, [column_shape], cleared, *halves, aliases={0: 0})
    height = rows * unknowns // LANES
    single, wide = ((2 * height, LANES), BF16), ((rows + 2 * height, LANES), BF16)
    partials = call(
        functools.partial(partial_kernel, unknowns),
        [((height, LANES), F32), wide, wide] + [single] * (n_by - 3),
        columns,
        co,
        ci,
        rx,
        ao,
        ai,
        *rest,
    )
    so = lax.ppermute(partials[1], "col", outer_pairs(n_by))
    others = [lax.ppermute(partials[d + 1], "col", shifted(n_by, d)) for d in range(2, n_by - 1)]
    si = lax.ppermute(partials[2], "col", inner_pairs(n_by))
    (acc,) = call(local_kernel, [((rows, n_core), F32)], res, inverse, spots, ao, ai)
    (out,) = call(functools.partial(final_kernel, unknowns), [((rows, n_core), BF16)], acc, member, spots, partials[0], so, si, *others)
    return out[:, None, None, :]


def solution(mesh):
    in_specs = (
        P("dev", "row", "col", None),
        P("dev", "row", "col", None),
        P(),
        P("row", "col", None, None),
        P("col", ("row", "dev")),
        P("row", "col", None),
        P("row", "col", None, None),
    )
    out_specs = P("dev", "row", "col", None)

    return jax.shard_map(per_device, mesh=mesh, in_specs=in_specs, out_specs=out_specs, check_vma=False)
```
